1024 devices in a mesh: temporal: 256 (over y, z, core), ulysses: 4 (over x).
Axes of the slice: x: 4, y: 8, z: 16, core: 2. Of those that a mesh axis runs over, the one named last changes fastest.
Arguments:
- queries: bfloat16 [262144, 1536], P(('temporal', 'ulysses')), may hold values from -12 to 12
- keys: bfloat16 [262144, 1536], P(('temporal', 'ulysses')), may hold values from -12 to 12
- values: bfloat16 [262144, 1536], P(('temporal', 'ulysses')), may hold values from -6 to 6
- tile_list: int32 [2048, 5], P('temporal'), may hold values from 0 to 2047, as said below
- counts: int32 [2048], P('temporal'), may hold values from 1 to 5, as said below
- out_weight: bfloat16 [1536, 1536], replicated, may hold values from -0.15625 to 0.15625
Outputs:
- projected: bfloat16 [262144, 1536], P(('temporal', 'ulysses'))
The draws below stay inside these ranges and needn't reach their ends.
Inputs may be any that keep to these rules, and one draw needn't show every extreme that they name: `tile_list`: every id in row g lies within 3 of g and in the same video as g; the first entry is g itself; the first counts[g] entries are distinct; entries past counts[g] equal g. `counts`: some tile has 5 live entries.
All inputs are finite; a program needn't handle non-finite values.
Results may differ from the reference program's by a relative error of at most 0.0056.
Values may be sent and summed in bfloat16 or wider, within the bound.
A program may use at most 64 MiB of HBM per device.

```python
import math
import jax
import jax.numpy as jnp
from jax import lax

D = 1536
HEADS = 12
HD = 128
TILE = 128
REACH = 3
MAXT = 5
TILES_T = 8
VID_GROUPS = 256
TOKENS = 262144
NT = 2048


def query_key_pair(key):
    base_key = jax.random.fold_in(key, 7)
    first_key, second_key = jax.random.split(base_key, 2)
    query_out = jax.random.truncated_normal(first_key, -6.0, 6.0, (TOKENS, D), jnp.float32)
    key_out = jax.random.truncated_normal(second_key, -6.0, 6.0, (TOKENS, D), jnp.float32)
    return (query_out, key_out)


def draw_queries(key, part):
    return query_key_pair(key)[0].astype(jnp.bfloat16)


def draw_keys(key, part):
    return query_key_pair(key)[1].astype(jnp.bfloat16)


def tile_lists(key):
    base_key = jax.random.fold_in(key, 11)
    cap_key, count_key, order_key = jax.random.split(base_key, 3)
    tiles = jnp.arange(NT, dtype=jnp.int32)
    video_tiles = VID_GROUPS * TILES_T
    shard_of = tiles // TILES_T
    shard_cap = jax.random.randint(cap_key, (NT // TILES_T,), 2, MAXT + 1)
    wanted = jnp.minimum(jax.random.randint(count_key, (NT,), 1, MAXT + 1), shard_cap[shard_of])
    wanted = jnp.where(tiles == TILES_T, MAXT, wanted)
    offsets = jnp.arange(-REACH, REACH + 1, dtype=jnp.int32)
    window = 2 * REACH + 1
    target = tiles[:, None] + offsets[None, :]
    inside = (target >= 0) & (target < NT) & (target // video_tiles == (tiles // video_tiles)[:, None])
    inside_count = jnp.sum(inside.astype(jnp.int32), axis=1)
    wanted = jnp.minimum(wanted, inside_count)
    ranking = jax.random.randint(order_key, (NT, window), 0, 1 << 20) * window + jnp.arange(window, dtype=jnp.int32)[None, :]
    ranking = jnp.where(offsets[None, :] == 0, -1, ranking)
    ranking = jnp.where(inside, ranking, ranking + (1 << 28))
    order = jnp.argsort(ranking, axis=1, stable=True)[:, :MAXT]
    chosen = jnp.take_along_axis(target, order, axis=1)
    slots = jnp.arange(MAXT, dtype=jnp.int32)[None, :]
    listed = jnp.where(slots < wanted[:, None], chosen, tiles[:, None])
    return (listed.astype(jnp.int32), wanted.astype(jnp.int32))


def draw_tile_list(key, part):
    return tile_lists(key)[0]


def draw_counts(key, part):
    return tile_lists(key)[1]


def shard_levels(stream_key, extent, cuts, least, high):
    factor_of, own = 1.0, jax.random.fold_in(stream_key, 6)
    for position, blocks in cuts:
        steps = jnp.exp(jax.random.uniform(jax.random.fold_in(own, position), (blocks,), jnp.float32, least / len(cuts), high / len(cuts)))
        factor_of = factor_of * jnp.repeat(steps, extent[position] // blocks).reshape([-1 if axis == position else 1 for axis in range(len(extent))])
    return factor_of


def centred(key, extent, spread, most, cuts=(), kind=jnp.bfloat16):
    entries = spread * jax.random.normal(key, extent, jnp.float32)
    if cuts:
        entries = entries * shard_levels(key, extent, cuts, -0.22, 0.18)
    return jnp.clip(entries, -most, most).astype(kind)


def setup_inputs(seed: int = 0) -> dict:
    key_list = jax.random.split(jax.random.key(seed), 7)
    queries = draw_queries(jax.random.fold_in(key_list[6], 71), 0)
    keys = draw_keys(jax.random.fold_in(key_list[6], 71), 0)
    values = centred(key_list[2], (TOKENS, D), 1.0, 6.0, ((0, 1024),))
    tile_list = draw_tile_list(jax.random.fold_in(key_list[6], 71), 0)
    counts = draw_counts(jax.random.fold_in(key_list[6], 71), 0)
    out_weight = centred(key_list[5], (D, D), D ** -0.5, 0.15625)
    return {"queries": queries, "keys": keys, "values": values, "tile_list": tile_list, "counts": counts, "out_weight": out_weight}


def reference(queries, keys, values, tile_list, counts, out_weight):
    query_all = queries.reshape(NT, TILE, HEADS, HD)
    key_all = keys.reshape(NT, TILE, HEADS, HD)
    value_all = values.reshape(NT, TILE, HEADS, HD)
    score_scale = 1.0 / math.sqrt(HD)
    slot_of = jnp.arange(MAXT * TILE, dtype=jnp.int32) // TILE

    def one_tile(tile_index):
        chosen = tile_list[tile_index]
        live = slot_of < counts[tile_index]
        query_tile = query_all[tile_index].astype(jnp.float32)
        key_rows = key_all[chosen].reshape(MAXT * TILE, HEADS, HD).astype(jnp.float32)
        value_rows = value_all[chosen].reshape(MAXT * TILE, HEADS, HD).astype(jnp.float32)
        scores = jnp.einsum('qhd,khd->hqk', query_tile, key_rows) * score_scale
        scores = jnp.where(live[None, None, :], scores, -jnp.inf)
        top = lax.optimization_barrier(jnp.max(scores, axis=-1, keepdims=True))
        weights = jnp.exp(scores - top)
        totals = lax.optimization_barrier(jnp.sum(weights, axis=-1, keepdims=True))
        rounded = lax.optimization_barrier(weights.astype(jnp.bfloat16)).astype(jnp.float32)
        mixed = jnp.einsum('hqk,khd->hqd', rounded, value_rows) / totals
        mixed = mixed.astype(jnp.bfloat16)
        return jnp.transpose(mixed, (1, 0, 2)).reshape(TILE, D)
    result = lax.map(one_tile, jnp.arange(NT, dtype=jnp.int32))
    attended = result.reshape(TOKENS, D)
    return jnp.dot(attended, out_weight, preferred_element_type=jnp.float32).astype(jnp.bfloat16)
```

```python
import functools
import math

import jax
import jax.numpy as jnp
from jax import lax
from jax.experimental import pallas as pl
from jax.experimental.pallas import tpu as pltpu
from jax.sharding import PartitionSpec as P

HD = 128
TILE = 128
REACH = 3
RING = 4
PAIR = 2
LOCAL_HEADS = 3
OWN = RING * PAIR
SPAN = OWN + 2 * REACH
SLOTS = 5
MESH = pl.DeviceIdType.MESH
NEG = -1e30
COLS = 256


def kernel(groups, tl_ref, cnt_ref, q_ref, k_ref, v_ref, w_ref, out_ref,
           kb0, kb1, kb2, vb0, vb1, vb2, qb0, qb1, qb2, ab0, ab1, ab2, ob0, ob1, ob2,
           wb0, wb1, wb2, to_right, to_left, acc, done,
           ssem, rsem, hssem, hrsem, lsem, wsem, osem):
    t = lax.axis_index("temporal")
    u = lax.axis_index("ulysses")
    right, left, far = lax.rem(u + 1, RING), lax.rem(u + 3, RING), lax.rem(u + 2, RING)
    after, before = lax.rem(t + 1, groups), lax.rem(t + groups - 1, groups)
    bufs = ((kb0, kb1, kb2), (vb0, vb1, vb2), (qb0, qb1, qb2))
    sources = (k_ref, v_ref, q_ref)
    joined, sent, weights = (ab0, ab1, ab2), (ob0, ob1, ob2), (wb0, wb1, wb2)

    def remote(src, dst, kind, index, device):
        return functools.partial(
            pltpu.make_async_remote_copy,
            src_ref=src, dst_ref=dst, send_sem=ssem.at[index, kind], recv_sem=rsem.at[index, kind],
            device_id=device, device_id_type=MESH)

    def columns(x, head):
        return pl.ds(pl.multiple_of((x * LOCAL_HEADS + head) * HD, HD), HD)

    def place(x):
        return pl.ds(pl.multiple_of(x * HD, HD), HD)

    def stage(s):
        head, kind = divmod(s, 3)
        base = REACH if kind < 2 else 0
        return sources[kind], bufs[kind][head], base, head

    def local_copy(s):
        src, buf, base, head = stage(s)
        return pltpu.make_async_copy(
            src.at[:, :, columns(u, head)], buf.at[pl.ds(base + PAIR * u, PAIR)], lsem.at[s])

    def weight_copy(head):
        return pltpu.make_async_copy(w_ref.at[:, head], weights[head], wsem.at[head])

    def first_hops(s, x):
        src, buf, base, head = stage(s)
        return (
            remote(src.at[0, :, columns(far, head)], to_right.at[s], 0, s, (t, right)),
            remote(src.at[1, :, columns(far, head)], to_left.at[s], 1, s, (t, left)),
            remote(src.at[:, :, columns(right, head)], buf.at[pl.ds(base + PAIR * x[0], PAIR)], 2, s, (t, right)),
            remote(src.at[:, :, columns(left, head)], buf.at[pl.ds(base + PAIR * x[1], PAIR)], 3, s, (t, left)),
        )

    def second_hops(s, x):
        src, buf, base, head = stage(s)
        return (
            remote(to_right.at[s], buf.at[base + PAIR * x[0]], 4, s, (t, right)),
            remote(to_left.at[s], buf.at[base + PAIR * x[1] + 1], 5, s, (t, left)),
        )

    def start(s):
        for copy in first_hops(s, (u, u)):
            copy().start()

    def relay(s):
        arrive = first_hops(s, (left, right))
        onward = second_hops(s, (left, right))
        for side in range(2):
            arrive[side]().wait_recv()
            onward[side]().start()

    def collect(s):
        arrive = first_hops(s, (left, right))
        arrive[2]().wait_recv()
        arrive[3]().wait_recv()
        for copy in second_hops(s, (far, far)):
            copy().wait_recv()
        local_copy(s).wait()

    def halo(head, kind):
        buf = bufs[kind][head]
        return tuple(
            functools.partial(
                pltpu.make_async_remote_copy,
                src_ref=buf.at[pl.ds(low, REACH)], dst_ref=buf.at[pl.ds(high, REACH)],
                send_sem=hssem.at[head, kind, side], recv_sem=hrsem.at[head, kind, side],
                device_id=(there, u), device_id_type=MESH)
            for side, (low, high, there) in enumerate(((OWN, 0, after), (REACH, REACH + OWN, before))))

    def halo_start(head, kind):
        for copy in halo(head, kind):
            copy().start()

    def halo_wait(head):
        for kind in range(2):
            for copy in halo(head, kind):
                copy().wait_recv()

    def out_first(head, x):
        s = 9 + head
        buf, dst = sent[head], joined[head]
        return (
            remote(buf.at[1, 0], to_right.at[s], 0, s, (t, right)),
            remote(buf.at[1, 1], to_left.at[s], 1, s, (t, left)),
            remote(buf.at[0], dst.at[:, :, place(x[0])], 2, s, (t, right)),
            remote(buf.at[2], dst.at[:, :, place(x[1])], 3, s, (t, left)),
        )

    def out_second(head, x):
        s = 9 + head
        dst = joined[head]
        return (
            remote(to_right.at[s], dst.at[0, :, place(x[0])], 4, s, (t, right)),
            remote(to_left.at[s], dst.at[1, :, place(x[1])], 5, s, (t, left)),
        )

    def out_start(head, parts):
        copies = out_first(head, (u, u))
        for part in parts:
            copies[part]().start()

    def out_relay(head):
        arrive = out_first(head, (left, right))
        onward = out_second(head, (left, right))
        for side in range(2):
            arrive[side]().wait_recv()
            onward[side]().start()

    def out_collect(head):
        arrive = out_first(head, (left, right))
        arrive[2]().wait_recv()
        arrive[3]().wait_recv()
        for copy in out_second(head, (far, far)):
            copy().wait_recv()

    first_tile = t * OWN - REACH
    rate = math.log2(math.e) / math.sqrt(HD)

    def attend(head, offset):
        kb, vb, qb = bufs[0][head], bufs[1][head], bufs[2][head]
        base = PAIR * lax.rem(u + offset, RING)
        row = lax.broadcasted_iota(jnp.int32, (1, SLOTS * TILE), 1)
        for i in range(PAIR):
            g = base + i
            ids = [jnp.clip(tl_ref[g, slot] - first_tile, 0, SPAN - 1) for slot in range(SLOTS)]
            key_rows = jnp.concatenate([kb[n] for n in ids], axis=0)
            scores = lax.dot_general(qb[g], key_rows, (((1,), (1,)), ((), ())),
                                     preferred_element_type=jnp.float32)
            scores = jnp.where(row < cnt_ref[g] * TILE, scores, NEG)
            top = jnp.max(scores, axis=-1, keepdims=True)
            parts = jnp.exp2((scores - top) * rate)
            totals = jnp.sum(parts, axis=-1, keepdims=True)
            value_rows = jnp.concatenate([vb[n] for n in ids], axis=0)
            mixed = jnp.dot(parts.astype(jnp.bfloat16), value_rows, preferred_element_type=jnp.float32)
            mixed = (mixed / totals).astype(jnp.bfloat16)
            if offset == 0:
                joined[head][i, :, place(u)] = mixed
            else:
                sent[head][offset - 1, i] = mixed

    def project(head):
        rows = joined[head][...].reshape(PAIR * TILE, RING * HD)

        def block(c, carry):
            cols = pl.ds(pl.multiple_of(c * COLS, COLS), COLS)
            w = weights[head][:, :, cols].reshape(RING * HD, COLS)
            part = jnp.dot(rows, w, preferred_element_type=jnp.float32)
            if head > 0:
                part = part + acc[:, cols]
            if head < LOCAL_HEADS - 1:
                acc[:, cols] = part
            else:
                done[:, cols] = part.astype(jnp.bfloat16)
            return carry

        lax.fori_loop(0, acc.shape[1] // COLS, block, 0)

    barrier = pltpu.get_barrier_semaphore()
    for device in ((t, right), (t, left), (after, u), (before, u)):
        pl.semaphore_signal(barrier, inc=1, device_id=device, device_id_type=MESH)
    for s in range(9):
        local_copy(s).start()
    for head in range(LOCAL_HEADS):
        weight_copy(head).start()
    pl.semaphore_wait(barrier, 4)

    start(0)
    start(1)
    relay(0)
    start(2)
    relay(1)
    start(3)
    collect(0)
    halo_start(0, 0)
    relay(2)
    start(4)
    collect(1)
    halo_start(0, 1)
    relay(3)
    start(5)
    collect(2)
    halo_wait(0)
    attend(0, 2)
    attend(0, 1)
    relay(4)
    start(6)
    collect(3)
    halo_start(1, 0)
    attend(0, 3)
    attend(0, 0)
    relay(5)
    start(7)
    out_start(0, (0, 1, 2, 3))
    collect(4)
    halo_start(1, 1)
    relay(6)
    start(8)
    out_relay(0)
    collect(5)
    halo_wait(1)
    attend(1, 2)
    attend(1, 1)
    relay(7)
    collect(6)
    halo_start(2, 0)
    attend(1, 3)
    attend(1, 0)
    relay(8)
    out_start(1, (0, 1, 2, 3))
    collect(7)
    halo_start(2, 1)
    weight_copy(0).wait()
    out_collect(0)
    project(0)
    collect(8)
    halo_wait(2)
    attend(2, 2)
    out_start(2, (0, 1))
    out_relay(1)
    attend(2, 1)
    out_start(2, (2,))
    attend(2, 3)
    out_start(2, (3,))
    out_relay(2)
    attend(2, 0)
    weight_copy(1).wait()
    out_collect(1)
    project(1)
    weight_copy(2).wait()
    out_collect(2)
    project(2)
    result = pltpu.make_async_copy(done, out_ref, osem)
    result.start()

    for s in range(9):
        for copy in first_hops(s, (u, u)) + second_hops(s, (left, right)):
            copy().wait_send()
    for head in range(LOCAL_HEADS):
        for copy in out_first(head, (u, u)) + out_second(head, (left, right)):
            copy().wait_send()
        for kind in range(2):
            for copy in halo(head, kind):
                copy().wait_send()
    result.wait()


def solution(mesh):
    groups = mesh.shape["temporal"]

    def on_device(queries, keys, values, tile_list, counts, out_weight):
        width = queries.shape[1]
        split = lambda a: a.reshape(PAIR, TILE, width)
        any_space = pl.BlockSpec(memory_space=pl.ANY)
        smem = pl.BlockSpec(memory_space=pltpu.SMEM)
        bf = jnp.bfloat16
        heads = range(LOCAL_HEADS)
        return pl.pallas_call(
            functools.partial(kernel, groups),
            out_shape=jax.ShapeDtypeStruct(queries.shape, bf),
            in_specs=[smem, smem, any_space, any_space, any_space, any_space],
            out_specs=any_space,
            scratch_shapes=(
                [pltpu.VMEM((SPAN, TILE, HD), bf) for _ in range(2) for _ in heads]
                + [pltpu.VMEM((OWN, TILE, HD), bf) for _ in heads]
                + [pltpu.VMEM((PAIR, TILE, RING * HD), bf) for _ in heads]
                + [pltpu.VMEM((RING - 1, PAIR, TILE, HD), bf) for _ in heads]
                + [pltpu.VMEM((RING, HD, width), bf) for _ in heads]
                + [pltpu.VMEM((12, TILE, HD), bf) for _ in range(2)]
                + [
                    pltpu.VMEM((PAIR * TILE, width), jnp.float32),
                    pltpu.VMEM((PAIR * TILE, width), bf),
                    pltpu.SemaphoreType.DMA((12, 6)),
                    pltpu.SemaphoreType.DMA((12, 6)),
                    pltpu.SemaphoreType.DMA((3, 2, 2)),
                    pltpu.SemaphoreType.DMA((3, 2, 2)),
                    pltpu.SemaphoreType.DMA((9,)),
                    pltpu.SemaphoreType.DMA((3,)),
                    pltpu.SemaphoreType.DMA,
                ]
            ),
            compiler_params=pltpu.CompilerParams(
                collective_id=0, has_side_effects=True, vmem_limit_bytes=56 * 1024 * 1024
            ),
        )(tile_list, counts, split(queries), split(keys), split(values),
          out_weight.reshape(RING, LOCAL_HEADS, HD, width))

    rows = P(("temporal", "ulysses"), None)
    return jax.shard_map(
        on_device,
        mesh=mesh,
        in_specs=(rows, rows, rows, P("temporal", None), P("temporal"), P()),
        out_specs=rows,
        check_vma=False,
    )
```

```python
import functools
import math

import jax
import jax.numpy as jnp
from jax import lax
from jax.experimental import pallas as pl
from jax.experimental.pallas import tpu as pltpu
from jax.sharding import PartitionSpec as P

HD = 128
TILE = 128
REACH = 3
RING = 4
PAIR = 2
LOCAL_HEADS = 3
OWN = RING * PAIR
SPAN = OWN + 2 * REACH
SLOTS = 5
MESH = pl.DeviceIdType.MESH
NEG = -1e30
COLS = 256
PLANE = 32


def kernel(groups, tl_ref, cnt_ref, q_ref, k_ref, v_ref, w_ref, out_ref,
           kb0, kb1, kb2, vb0, vb1, vb2, qb0, qb1, qb2, ab0, ab1, ab2, ob0, ob1, ob2,
           wb0, wb1, wb2, to_right, to_left, acc, done,
           ssem, rsem, hssem, hrsem, lsem, wsem, osem, ack):
    t = lax.axis_index("temporal")
    u = lax.axis_index("ulysses")
    right, left, far = lax.rem(u + 1, RING), lax.rem(u + 3, RING), lax.rem(u + 2, RING)
    after, before = lax.rem(t + 1, groups), lax.rem(t + groups - 1, groups)
    bufs = ((kb0, kb1, kb2), (vb0, vb1, vb2), (qb0, qb1, qb2))
    sources = (k_ref, v_ref, q_ref)
    joined, sent, weights = (ab0, ab1, ab2), (ob0, ob1, ob2), (wb0, wb1, wb2)

    def remote(src, dst, kind, index, device):
        return functools.partial(
            pltpu.make_async_remote_copy,
            src_ref=src, dst_ref=dst, send_sem=ssem.at[index, kind], recv_sem=rsem.at[index, kind],
            device_id=device, device_id_type=MESH)

    def columns(x, head):
        return pl.ds(pl.multiple_of((x * LOCAL_HEADS + head) * HD, HD), HD)

    def place(x):
        return pl.ds(pl.multiple_of(x * HD, HD), HD)

    def stage(s):
        head, kind = divmod(s, 3)
        base = REACH if kind < 2 else 0
        return sources[kind], bufs[kind][head], base, head

    def local_copy(s):
        src, buf, base, head = stage(s)
        return pltpu.make_async_copy(
            src.at[:, :, columns(u, head)], buf.at[pl.ds(base + PAIR * u, PAIR)], lsem.at[s])

    def weight_copy(head):
        return pltpu.make_async_copy(w_ref.at[:, head], weights[head], wsem.at[head])

    def first_hops(s, x):
        src, buf, base, head = stage(s)
        return (
            remote(src.at[0, :, columns(far, head)], to_right.at[s], 0, s, (t, right)),
            remote(src.at[1, :, columns(far, head)], to_left.at[s], 1, s, (t, left)),
            remote(src.at[:, :, columns(right, head)], buf.at[pl.ds(base + PAIR * x[0], PAIR)], 2, s, (t, right)),
            remote(src.at[:, :, columns(left, head)], buf.at[pl.ds(base + PAIR * x[1], PAIR)], 3, s, (t, left)),
        )

    def second_hops(s, x):
        src, buf, base, head = stage(s)
        return (
            remote(to_right.at[s], buf.at[base + PAIR * x[0]], 4, s, (t, right)),
            remote(to_left.at[s], buf.at[base + PAIR * x[1] + 1], 5, s, (t, left)),
        )

    def start(s):
        for copy in first_hops(s, (u, u)):
            copy().start()

    def relay(s):
        arrive = first_hops(s, (left, right))
        onward = second_hops(s, (left, right))
        for side in range(2):
            arrive[side]().wait_recv()
            onward[side]().start()

    def collect(s):
        arrive = first_hops(s, (left, right))
        arrive[2]().wait_recv()
        arrive[3]().wait_recv()
        for copy in second_hops(s, (far, far)):
            copy().wait_recv()
        local_copy(s).wait()

    def halo(head, kind):
        buf = bufs[kind][head]
        return tuple(
            functools.partial(
                pltpu.make_async_remote_copy,
                src_ref=buf.at[pl.ds(low, REACH)], dst_ref=buf.at[pl.ds(high, REACH)],
                send_sem=hssem.at[head, kind, side], recv_sem=hrsem.at[head, kind, side],
                device_id=(there, u), device_id_type=MESH)
            for side, (low, high, there) in enumerate(((OWN, 0, after), (REACH, REACH + OWN, before))))

    def halo_start(head, kind):
        for copy in halo(head, kind):
            copy().start()

    def halo_wait(head):
        for kind in range(2):
            for copy in halo(head, kind):
                copy().wait_recv()

    def out_first(head, x):
        s = 9 + head
        buf, dst = sent[head], joined[head]
        return (
            remote(buf.at[1, 0], to_right.at[s], 0, s, (t, right)),
            remote(buf.at[1, 1], to_left.at[s], 1, s, (t, left)),
            remote(buf.at[0], dst.at[:, :, place(x[0])], 2, s, (t, right)),
            remote(buf.at[2], dst.at[:, :, place(x[1])], 3, s, (t, left)),
        )

    def out_second(head, x):
        s = 9 + head
        dst = joined[head]
        return (
            remote(to_right.at[s], dst.at[0, :, place(x[0])], 4, s, (t, right)),
            remote(to_left.at[s], dst.at[1, :, place(x[1])], 5, s, (t, left)),
        )

    def out_start(head, parts):
        copies = out_first(head, (u, u))
        for part in parts:
            copies[part]().start()

    def out_relay(head):
        arrive = out_first(head, (left, right))
        onward = out_second(head, (left, right))
        for side in range(2):
            arrive[side]().wait_recv()
            onward[side]().start()

    def out_collect(head):
        arrive = out_first(head, (left, right))
        arrive[2]().wait_recv()
        arrive[3]().wait_recv()
        for copy in out_second(head, (far, far)):
            copy().wait_recv()

    first_tile = t * OWN - REACH
    rate = math.log2(math.e) / math.sqrt(HD)

    def attend(head, offset):
        kb, vb, qb = bufs[0][head], bufs[1][head], bufs[2][head]
        base = PAIR * lax.rem(u + offset, RING)
        row = lax.broadcasted_iota(jnp.int32, (1, SLOTS * TILE), 1)
        for i in range(PAIR):
            g = base + i
            ids = [jnp.clip(tl_ref[g, slot] - first_tile, 0, SPAN - 1) for slot in range(SLOTS)]
            key_rows = jnp.concatenate([kb[n] for n in ids], axis=0)
            scores = lax.dot_general(qb[g], key_rows, (((1,), (1,)), ((), ())),
                                     preferred_element_type=jnp.float32)
            scores = jnp.where(row < cnt_ref[g] * TILE, scores, NEG)
            top = jnp.max(scores, axis=-1, keepdims=True)
            parts = jnp.exp2((scores - top) * rate)
            totals = jnp.sum(parts, axis=-1, keepdims=True)
            value_rows = jnp.concatenate([vb[n] for n in ids], axis=0)
            mixed = jnp.dot(parts.astype(jnp.bfloat16), value_rows, preferred_element_type=jnp.float32)
            mixed = (mixed / totals).astype(jnp.bfloat16)
            if offset == 0:
                joined[head][i, :, place(u)] = mixed
            else:
                sent[head][offset - 1, i] = mixed

    def project(head):
        rows = joined[head][...].reshape(PAIR * TILE, RING * HD)

        def block(c, carry):
            cols = pl.ds(pl.multiple_of(c * COLS, COLS), COLS)
            w = weights[head][:, :, cols].reshape(RING * HD, COLS)
            part = jnp.dot(rows, w, preferred_element_type=jnp.float32)
            if head > 0:
                part = part + acc[:, cols]
            if head < LOCAL_HEADS - 1:
                acc[:, cols] = part
            else:
                done[:, cols] = part.astype(jnp.bfloat16)
            return carry

        lax.fori_loop(0, acc.shape[1] // COLS, block, 0)

    plane = min(PLANE, groups)
    spot = lax.rem(t, plane)
    head_of = lax.div(plane - 1 - spot, plane - 1)
    second = lax.div(plane - 1 - lax.rem(spot + plane - 1, plane), plane - 1)
    tail_of = lax.div(spot, plane - 1)
    up, down = 1 - head_of - tail_of, head_of + second
    barrier = pltpu.get_barrier_semaphore()

    def tell(sem, device):
        pl.semaphore_signal(sem, inc=1, device_id=device, device_id_type=MESH)

    tell(barrier, (t, right))
    tell(barrier, (t, left))
    for flag, there in ((up, after), (down, before)):
        pl.when(flag == 1)(functools.partial(tell, barrier, (there, u)))
    for s in range(9):
        local_copy(s).start()
    pl.semaphore_wait(barrier, 4 - up - down)

    start(0)
    start(1)
    for flag, there in ((up, after), (down, before)):
        pl.when(flag == 0)(functools.partial(tell, ack, (there, u)))
    for head in range(LOCAL_HEADS):
        weight_copy(head).start()
    relay(0)
    start(2)
    relay(1)
    start(3)
    collect(0)

    @pl.when(up + down > 0)
    def _():
        pl.semaphore_wait(ack, up + down)

    halo_start(0, 0)
    relay(2)
    start(4)
    collect(1)
    halo_start(0, 1)
    relay(3)
    start(5)
    collect(2)
    halo_wait(0)
    attend(0, 2)
    attend(0, 1)
    relay(4)
    start(6)
    collect(3)
    halo_start(1, 0)
    attend(0, 3)
    attend(0, 0)
    relay(5)
    start(7)
    out_start(0, (0, 1, 2, 3))
    collect(4)
    halo_start(1, 1)
    relay(6)
    start(8)
    out_relay(0)
    collect(5)
    halo_wait(1)
    attend(1, 2)
    attend(1, 1)
    relay(7)
    collect(6)
    halo_start(2, 0)
    attend(1, 3)
    attend(1, 0)
    relay(8)
    out_start(1, (0, 1, 2, 3))
    collect(7)
    halo_start(2, 1)
    weight_copy(0).wait()
    out_collect(0)
    project(0)
    collect(8)
    halo_wait(2)
    attend(2, 2)
    out_start(2, (0, 1))
    out_relay(1)
    attend(2, 1)
    out_start(2, (2,))
    attend(2, 3)
    out_start(2, (3,))
    out_relay(2)
    attend(2, 0)
    weight_copy(1).wait()
    out_collect(1)
    project(1)
    weight_copy(2).wait()
    out_collect(2)
    project(2)
    result = pltpu.make_async_copy(done, out_ref, osem)
    result.start()

    for s in range(9):
        for copy in first_hops(s, (u, u)) + second_hops(s, (left, right)):
            copy().wait_send()
    for head in range(LOCAL_HEADS):
        for copy in out_first(head, (u, u)) + out_second(head, (left, right)):
            copy().wait_send()
        for kind in range(2):
            for copy in halo(head, kind):
                copy().wait_send()
    result.wait()


def solution(mesh):
    groups = mesh.shape["temporal"]

    def on_device(queries, keys, values, tile_list, counts, out_weight):
        width = queries.shape[1]
        split = lambda a: a.reshape(PAIR, TILE, width)
        any_space = pl.BlockSpec(memory_space=pl.ANY)
        smem = pl.BlockSpec(memory_space=pltpu.SMEM)
        bf = jnp.bfloat16
        heads = range(LOCAL_HEADS)
        return pl.pallas_call(
            functools.partial(kernel, groups),
            out_shape=jax.ShapeDtypeStruct(queries.shape, bf),
            in_specs=[smem, smem, any_space, any_space, any_space, any_space],
            out_specs=any_space,
            scratch_shapes=(
                [pltpu.VMEM((SPAN, TILE, HD), bf) for _ in range(2) for _ in heads]
                + [pltpu.VMEM((OWN, TILE, HD), bf) for _ in heads]
                + [pltpu.VMEM((PAIR, TILE, RING * HD), bf) for _ in heads]
                + [pltpu.VMEM((RING - 1, PAIR, TILE, HD), bf) for _ in heads]
                + [pltpu.VMEM((RING, HD, width), bf) for _ in heads]
                + [pltpu.VMEM((12, TILE, HD), bf) for _ in range(2)]
                + [
                    pltpu.VMEM((PAIR * TILE, width), jnp.float32),
                    pltpu.VMEM((PAIR * TILE, width), bf),
                    pltpu.SemaphoreType.DMA((12, 6)),
                    pltpu.SemaphoreType.DMA((12, 6)),
                    pltpu.SemaphoreType.DMA((3, 2, 2)),
                    pltpu.SemaphoreType.DMA((3, 2, 2)),
                    pltpu.SemaphoreType.DMA((9,)),
                    pltpu.SemaphoreType.DMA((3,)),
                    pltpu.SemaphoreType.DMA,
                    pltpu.SemaphoreType.REGULAR,
                ]
            ),
            compiler_params=pltpu.CompilerParams(
                collective_id=0, has_side_effects=True, vmem_limit_bytes=56 * 1024 * 1024
            ),
        )(tile_list, counts, split(queries), split(keys), split(values),
          out_weight.reshape(RING, LOCAL_HEADS, HD, width))

    rows = P(("temporal", "ulysses"), None)
    return jax.shard_map(
        on_device,
        mesh=mesh,
        in_specs=(rows, rows, rows, P("temporal", None), P("temporal"), P()),
        out_specs=rows,
        check_vma=False,
    )
```

```python
import functools
import math

import jax
import jax.numpy as jnp
from jax import lax
from jax.experimental import pallas as pl
from jax.experimental.pallas import tpu as pltpu
from jax.sharding import PartitionSpec as P

HD = 128
TILE = 128
REACH = 3
RING = 4
PAIR = 2
LOCAL_HEADS = 3
OWN = RING * PAIR
SPAN = OWN + 2 * REACH
SLOTS = 5
MESH = pl.DeviceIdType.MESH
NEG = -1e30
COLS = 256
BLOCKS = 6
PLANE = 32
ORDER = ((0, 0), (0, 1), (1, 0), (1, 1), (2, 0), (2, 1), (0, 2), (1, 2), (2, 2))


def kernel(groups, tl_ref, cnt_ref, q_ref, k_ref, v_ref, w_ref, out_ref,
           kb0, kb1, kb2, vb0, vb1, vb2, qb0, qb1, qb2, ab0, ab1, ab2, ob0, ob1, ob2,
           wb0, wb1, wb2, acc, done,
           ssem, rsem, hssem, hrsem, lsem, wsem, osem, ack):
    t = lax.axis_index("temporal")
    u = lax.axis_index("ulysses")
    right, left, far = lax.rem(u + 1, RING), lax.rem(u + 3, RING), lax.rem(u + 2, RING)
    after, before = lax.rem(t + 1, groups), lax.rem(t + groups - 1, groups)
    bufs = ((kb0, kb1, kb2), (vb0, vb1, vb2), (qb0, qb1, qb2))
    sources = (k_ref, v_ref, q_ref)
    joined, sent, weights = (ab0, ab1, ab2), (ob0, ob1, ob2), (wb0, wb1, wb2)

    def remote(src, dst, kind, index, device):
        return functools.partial(
            pltpu.make_async_remote_copy,
            src_ref=src, dst_ref=dst, send_sem=ssem.at[index, kind], recv_sem=rsem.at[index, kind],
            device_id=device, device_id_type=MESH)

    def columns(x, head):
        return pl.ds(pl.multiple_of((x * LOCAL_HEADS + head) * HD, HD), HD)

    def place(x):
        return pl.ds(pl.multiple_of(x * HD, HD), HD)

    def stage(s):
        head, kind = ORDER[s]
        base = REACH if kind < 2 else 0
        return sources[kind], bufs[kind][head], base, head

    def local_copy(s):
        src, buf, base, head = stage(s)
        return pltpu.make_async_copy(
            src.at[:, :, columns(u, head)], buf.at[pl.ds(base + PAIR * u, PAIR)], lsem.at[s])

    def weight_copy(head):
        return pltpu.make_async_copy(w_ref.at[:, head], weights[head], wsem.at[head])

    def sends(s, x):
        src, buf, base, head = stage(s)
        return (
            remote(src.at[0, :, columns(far, head)], buf.at[base + PAIR * x[0]], 0, s, (t, far)),
            remote(src.at[1, :, columns(far, head)], buf.at[base + PAIR * x[0] + 1], 1, s, (t, far)),
            remote(src.at[:, :, columns(right, head)], buf.at[pl.ds(base + PAIR * x[1], PAIR)], 2, s, (t, right)),
            remote(src.at[:, :, columns(left, head)], buf.at[pl.ds(base + PAIR * x[2], PAIR)], 3, s, (t, left)),
        )

    def collect(s):
        for copy in sends(s, (far, left, right)):
            copy().wait_recv()
        local_copy(s).wait()

    def halo(head, kind):
        buf = bufs[kind][head]
        return tuple(
            functools.partial(
                pltpu.make_async_remote_copy,
                src_ref=buf.at[pl.ds(low, REACH)], dst_ref=buf.at[pl.ds(high, REACH)],
                send_sem=hssem.at[head, kind, side], recv_sem=hrsem.at[head, kind, side],
                device_id=(there, u), device_id_type=MESH)
            for side, (low, high, there) in enumerate(((OWN, 0, after), (REACH, REACH + OWN, before))))

    def halo_wait(head):
        for kind in range(2):
            for copy in halo(head, kind):
                copy().wait_recv()

    def out_sends(head, x):
        s = 9 + head
        buf, dst = sent[head], joined[head]
        return (
            remote(buf.at[1, 0], dst.at[0, :, place(x[0])], 0, s, (t, far)),
            remote(buf.at[1, 1], dst.at[1, :, place(x[0])], 1, s, (t, far)),
            remote(buf.at[0], dst.at[:, :, place(x[1])], 2, s, (t, right)),
            remote(buf.at[2], dst.at[:, :, place(x[2])], 3, s, (t, left)),
        )

    def out_start(head, parts):
        copies = out_sends(head, (u, u, u))
        for part in parts:
            copies[part]().start()

    def out_collect(head):
        for copy in out_sends(head, (far, left, right)):
            copy().wait_recv()

    first_tile = t * OWN - REACH
    rate = math.log2(math.e) / math.sqrt(HD)

    def attend(head, offset):
        kb, vb, qb = bufs[0][head], bufs[1][head], bufs[2][head]
        base = PAIR * lax.rem(u + offset, RING)
        row = lax.broadcasted_iota(jnp.int32, (1, SLOTS * TILE), 1)
        for i in range(PAIR):
            g = base + i
            ids = [jnp.clip(tl_ref[g, slot] - first_tile, 0, SPAN - 1) for slot in range(SLOTS)]
            key_rows = jnp.concatenate([kb[n] for n in ids], axis=0)
            scores = lax.dot_general(qb[g], key_rows, (((1,), (1,)), ((), ())),
                                     preferred_element_type=jnp.float32)
            scores = jnp.where(row < cnt_ref[g] * TILE, scores, NEG)
            top = jnp.max(scores, axis=-1, keepdims=True)
            parts = jnp.exp2((scores - top) * rate)
            totals = jnp.sum(parts, axis=-1, keepdims=True)
            value_rows = jnp.concatenate([vb[n] for n in ids], axis=0)
            mixed = jnp.dot(parts.astype(jnp.bfloat16), value_rows, preferred_element_type=jnp.float32)
            mixed = (mixed / totals).astype(jnp.bfloat16)
            if offset == 0:
                joined[head][i, :, place(u)] = mixed
            else:
                sent[head][offset - 1, i] = mixed

    def project(head):
        rows = joined[head][...].reshape(PAIR * TILE, RING * HD)

        def product(c):
            cols = pl.ds(pl.multiple_of(c * COLS, COLS), COLS)
            w = weights[head][:, :, cols].reshape(RING * HD, COLS)
            return cols, jnp.dot(rows, w, preferred_element_type=jnp.float32)

        def block(c, carry):
            cols, part = product(c)
            acc[:, cols] = part + acc[:, cols] if head > 0 else part
            return carry

        if head < LOCAL_HEADS - 1:
            lax.fori_loop(0, BLOCKS, block, 0)
            return
        for c in range(BLOCKS):
            cols, part = product(c)
            done[:, cols] = (part + acc[:, cols]).astype(jnp.bfloat16)
            result(c).start()

    def result(c):
        cols = pl.ds(c * COLS, COLS)
        return pltpu.make_async_copy(done.at[:, cols], out_ref.at[:, cols], osem.at[c])

    plane = min(PLANE, groups)
    spot = lax.rem(t, plane)
    head_of = lax.div(plane - 1 - spot, plane - 1)
    second = lax.div(plane - 1 - lax.rem(spot + plane - 1, plane), plane - 1)
    tail_of = lax.div(spot, plane - 1)
    up, down = 1 - head_of - tail_of, head_of + second
    barrier = pltpu.get_barrier_semaphore()

    def tell(sem, device):
        pl.semaphore_signal(sem, inc=1, device_id=device, device_id_type=MESH)

    tell(barrier, (t, right))
    tell(barrier, (t, left))
    tell(barrier, (t, far))
    for flag, there in ((up, after), (down, before)):
        pl.when(flag == 1)(functools.partial(tell, barrier, (there, u)))
    for s in range(9):
        local_copy(s).start()
    pl.semaphore_wait(barrier, 5 - up - down)

    for s in range(9):
        for copy in sends(s, (u, u, u)):
            copy().start()
    for flag, there in ((up, after), (down, before)):
        pl.when(flag == 0)(functools.partial(tell, ack, (there, u)))
    for head in range(LOCAL_HEADS):
        weight_copy(head).start()
    for s in range(9):
        head, kind = ORDER[s]
        collect(s)
        if s == 0:
            @pl.when(up + down > 0)
            def _():
                pl.semaphore_wait(ack, up + down)
        if kind < 2:
            for copy in halo(head, kind):
                copy().start()
            continue
        halo_wait(head)
        attend(head, 2)
        out_start(head, (0, 1))
        attend(head, 1)
        out_start(head, (2,))
        attend(head, 3)
        out_start(head, (3,))
        attend(head, 0)
    for head in range(LOCAL_HEADS):
        weight_copy(head).wait()
        out_collect(head)
        project(head)

    for s in range(9):
        for copy in sends(s, (u, u, u)):
            copy().wait_send()
    for head in range(LOCAL_HEADS):
        for copy in out_sends(head, (u, u, u)):
            copy().wait_send()
        for kind in range(2):
            for copy in halo(head, kind):
                copy().wait_send()
    for c in range(BLOCKS):
        result(c).wait()


def solution(mesh):
    groups = mesh.shape["temporal"]

    def on_device(queries, keys, values, tile_list, counts, out_weight):
        width = queries.shape[1]
        split = lambda a: a.reshape(PAIR, TILE, width)
        any_space = pl.BlockSpec(memory_space=pl.ANY)
        smem = pl.BlockSpec(memory_space=pltpu.SMEM)
        bf = jnp.bfloat16
        heads = range(LOCAL_HEADS)
        return pl.pallas_call(
            functools.partial(kernel, groups),
            out_shape=jax.ShapeDtypeStruct(queries.shape, bf),
            in_specs=[smem, smem, any_space, any_space, any_space, any_space],
            out_specs=any_space,
            scratch_shapes=(
                [pltpu.VMEM((SPAN, TILE, HD), bf) for _ in range(2) for _ in heads]
                + [pltpu.VMEM((OWN, TILE, HD), bf) for _ in heads]
                + [pltpu.VMEM((PAIR, TILE, RING * HD), bf) for _ in heads]
                + [pltpu.VMEM((RING - 1, PAIR, TILE, HD), bf) for _ in heads]
                + [pltpu.VMEM((RING, HD, width), bf) for _ in heads]
                + [
                    pltpu.VMEM((PAIR * TILE, width), jnp.float32),
                    pltpu.VMEM((PAIR * TILE, width), bf),
                    pltpu.SemaphoreType.DMA((12, 4)),
                    pltpu.SemaphoreType.DMA((12, 4)),
                    pltpu.SemaphoreType.DMA((3, 2, 2)),
                    pltpu.SemaphoreType.DMA((3, 2, 2)),
                    pltpu.SemaphoreType.DMA((9,)),
                    pltpu.SemaphoreType.DMA((3,)),
                    pltpu.SemaphoreType.DMA((BLOCKS,)),
                    pltpu.SemaphoreType.REGULAR,
                ]
            ),
            compiler_params=pltpu.CompilerParams(
                collective_id=0, has_side_effects=True, vmem_limit_bytes=56 * 1024 * 1024
            ),
        )(tile_list, counts, split(queries), split(keys), split(values),
          out_weight.reshape(RING, LOCAL_HEADS, HD, width))

    rows = P(("temporal", "ulysses"), None)
    return jax.shard_map(
        on_device,
        mesh=mesh,
        in_specs=(rows, rows, rows, P("temporal", None), P("temporal"), P()),
        out_specs=rows,
        check_vma=False,
    )
```
